32 devices in a mesh: groups: 2 (over x), row: 8 (over z, y), col: 2 (over core).
Axes of the slice: x: 2, y: 2, z: 4, core: 2. Of those that a mesh axis runs over, the one named last changes fastest.
Arguments:
- positions: float32 [32768, 384], P(('groups', 'row', 'col')), parts along dimension 0, may hold values from -1 to 1
- momenta: float32 [32768, 384], P(('groups', 'row', 'col')), parts along dimension 0, may hold values from -3 to 3
- tile_values: bfloat16 [3072, 128, 128], P(('groups', 'row', 'col')), parts along dimension 0, may hold values from -0.19921875 to 0.19921875
- tile_rows: int32 [3072], P(('groups', 'row', 'col')), parts along dimension 0, may hold values from 0 to 7
- tile_cols: int32 [3072], P(('groups', 'row', 'col')), parts along dimension 0, may hold values from 0 to 23
- tile_count: int32 [32], P(('groups', 'row', 'col')), parts along dimension 0, may hold values from 24 to 96, as said below
- channel_coupling: bfloat16 [48, 48], replicated, may hold values from -0.875 to 0.875
Outputs:
- new_positions: float32 [32768, 384], P(('groups', 'row', 'col')), parts along dimension 0
- new_momenta: float32 [32768, 384], P(('groups', 'row', 'col')), parts along dimension 0
- energy: float32 [16], P('groups'), parts along dimension 0
The draws below stay inside these ranges and needn't reach their ends.
There are 2 independent parts, one for each index of `groups`. The reference program is written for one: setup_inputs(seed, part) draws one part's arguments, and reference() takes and returns one part's arrays. A program takes and returns all parts, laid end to end along the dimension named above; an argument that names none is the same for every part. Nothing has to cross between parts.
Inputs may be any that keep to these rules, and one draw needn't show every extreme that they name: tile_count[b] is the number of live slots of block b; slots at or past it are ignored; some block has exactly 96 live slots.
All inputs are finite; a program needn't handle non-finite values.
Results may differ from the reference program's by a relative error of at most 0.00079.
Values may be sent and summed in bfloat16 or wider, within the bound.
A program may use at most 64 MiB of HBM per device.

```python
import jax
import jax.numpy as jnp
from jax import lax

CH = 48
REP = 8
TILE = 128
STEPS = 2
TPD = 8
MAXT = 96
BLOCKS = 16
CELLS = 16384
ALLT = 1536


def draw_tile_count(key, part):
    counts = jax.random.randint(key, (BLOCKS,), MAXT // 4, MAXT + 1)
    chosen = jax.random.randint(jax.random.fold_in(key, 17), (), 0, BLOCKS)
    return jnp.where(jnp.arange(BLOCKS) == chosen, MAXT, counts).astype(jnp.int32)


def plant(result, rng, least, high):
    longest = result.shape.index(max(result.shape))
    spots = []
    for shift in (0, 1):
        where = [jax.random.randint(jax.random.fold_in(rng, axis), (), 0, length) for axis, length in enumerate(result.shape)]
        where[longest] = (where[longest] + shift) % result.shape[longest]
        spots.append(tuple(where))
    return result.at[spots[0]].set(least).at[spots[1]].set(high)


def steps_of(key, dims, shards, least, high):
    factor_of = 1.0
    for position, parts in shards:
        heights = jax.random.uniform(jax.random.fold_in(jax.random.fold_in(key, 6), position), (parts,), jnp.float32, least / len(shards), high / len(shards))
        factor_of = factor_of * jnp.repeat(jnp.exp(heights), dims[position] // parts).reshape((-1,) + (1,) * (len(dims) - 1 - position))
    return factor_of


def bell_draw(own_key, extent, scale, bound, split=(), held_as=jnp.bfloat16):
    entries = scale * jax.random.normal(own_key, extent, jnp.float32)
    if split:
        entries = entries * steps_of(own_key, extent, split, -0.22, 0.18)
    return jnp.clip(entries, -bound, bound).astype(held_as)


def setup_inputs(seed: int = 0, part: int = 0) -> dict:
    seeds = jax.random.split(jax.random.key(seed), 8)
    part_splits = jax.random.split(jax.random.fold_in(seeds[7], part), 8)
    positions = jnp.clip(jax.random.uniform(part_splits[0], (CELLS, REP * CH), jnp.float32, -1.0, 1.0) * steps_of(part_splits[0], (CELLS, REP * CH), ((0, 16),), -0.4, 0.0), -1.0, 1.0)
    momenta = bell_draw(part_splits[1], (CELLS, REP * CH), 0.5, 3.0, ((0, 16),), jnp.float32)
    tile_values = bell_draw(part_splits[2], (ALLT, TILE, TILE), 0.03, 0.19921875, ((0, 16),))
    tile_rows = plant(jax.random.randint(part_splits[3], (ALLT,), 0, TPD), jax.random.fold_in(part_splits[3], 1), 0, TPD - 1).astype(jnp.int32)
    tile_cols = plant(jax.random.randint(part_splits[4], (ALLT,), 0, 3 * TPD), jax.random.fold_in(part_splits[4], 1), 0, (3 * TPD) - 1).astype(jnp.int32)
    tile_count = draw_tile_count(jax.random.fold_in(jax.random.fold_in(seeds[7], part), 71), part)
    channel_coupling = bell_draw(seeds[6], (CH, CH), CH ** -0.5, 0.875)
    return {"positions": positions, "momenta": momenta, "tile_values": tile_values, "tile_rows": tile_rows, "tile_cols": tile_cols, "tile_count": tile_count, "channel_coupling": channel_coupling}


def plan_field(rounded, tile_values, tile_rows, tile_cols, tile_count):
    width = rounded.shape[1]
    source_tiles = rounded.reshape(BLOCKS * TPD, TILE, width).astype(jnp.float32)
    values = tile_values.reshape(BLOCKS, MAXT, TILE, TILE)
    rows = tile_rows.reshape(BLOCKS, MAXT)
    cols = tile_cols.reshape(BLOCKS, MAXT)

    def one_block(index):
        block = index.astype(jnp.int32)
        source_index = (block * TPD - TPD + cols[block]) % (BLOCKS * TPD)
        sources = source_tiles[source_index]
        products = jnp.einsum('sij,sjk->sik', values[block].astype(jnp.float32), sources, precision=lax.Precision.HIGHEST)
        live = jnp.arange(MAXT, dtype=jnp.int32) < tile_count[block]
        place = ((rows[block][None, :] == jnp.arange(TPD, dtype=jnp.int32)[:, None]) & live[None, :]).astype(jnp.float32)
        return jnp.einsum('ts,sik->tik', place, products, precision=lax.Precision.HIGHEST)
    fields = lax.map(one_block, jnp.arange(BLOCKS, dtype=jnp.int32))
    return fields.reshape(BLOCKS * TPD * TILE, width)

def reference(positions, momenta, tile_values, tile_rows, tile_cols, tile_count, channel_coupling):
    x_state = positions
    y_state = momenta
    coupling = channel_coupling.astype(jnp.float32)
    energy = jnp.zeros((REP,), jnp.float32)
    for step in range(STEPS):
        rounded = x_state.astype(jnp.bfloat16)
        field = plan_field(rounded, tile_values, tile_rows, tile_cols, tile_count)
        interference = field.astype(jnp.bfloat16).astype(jnp.float32).reshape(CELLS, REP, CH)
        mixed = jnp.einsum('crb,ba->cra', interference, coupling, precision=lax.Precision.HIGHEST).reshape(CELLS, REP * CH)
        totals = lax.optimization_barrier(jnp.sum(x_state.reshape(CELLS, REP, CH), axis=2, keepdims=True))
        penalty = jnp.broadcast_to(0.02 * (totals - (2.0 - CH)), (CELLS, REP, CH)).reshape(CELLS, REP * CH)
        detune = 1.0 - (step + 1.0) / (STEPS + 1.0)
        y_state = y_state + 0.5 * (-detune * x_state - 0.4 * (mixed + penalty))
        if step == STEPS - 1:
            weighted = rounded.astype(jnp.float32) * mixed
            energy = lax.optimization_barrier(jnp.sum(weighted.reshape(CELLS, REP, CH), axis=(0, 2))) / jnp.sqrt(jnp.float32(CELLS * CH))
        x_state = jnp.clip(x_state + 0.5 * y_state, -1.0, 1.0)
    return (x_state, y_state, energy)
```

```python
import functools

import jax
import jax.numpy as jnp
from jax import lax
from jax.experimental import pallas as pl
from jax.experimental.pallas import tpu as pltpu
from jax.sharding import PartitionSpec as P

STEPS = 2
LANES = 128
HALVES = 2
MESH = pl.DeviceIdType.MESH
F32 = jnp.float32
BF16 = jnp.bfloat16


def group_index(index, channels, replicas):
    group = jnp.zeros(index.shape, jnp.int32)
    for r in range(1, replicas):
        group = group + (index >= r * channels).astype(jnp.int32)
    return group


def main_kernel(
    rows_n, cols_n, channels, scale,
    count_hbm, rows_hbm, cols_hbm, coupling_hbm, x_hbm, y_hbm, v_hbm,
    xb, yb, e_out,
    win0, win1, values, sums, dense_hi, dense_lo, field, mixed_ref, mix, ones, epart, eall,
    count_ref, rows_ref, cols_ref, coupling_ref, keys, prev_v, last_v, prev_ref, last_ref,
    in_sem, small_sem, table_sem, send_sem, recv_sem, esend_sem, erecv_sem,
):
    cells, width = xb.shape
    slots, tile, _ = values.shape
    chunk = 2 * tile
    chunks = cells // chunk
    targets = cells // tile
    sources = 3 * targets
    replicas = width // channels
    groups = width // LANES
    half = cells // HALVES
    n = rows_n * cols_n
    wins = (win0, win1)
    row, col = lax.axis_index("row"), lax.axis_index("col")
    me = row * cols_n + col

    def device(flat):
        return {"row": lax.div(flat, cols_n), "col": lax.rem(flat, cols_n)}

    def lanes_of(first, last):
        return pl.ds(first * LANES, (last - first) * LANES)

    def x_copy(g):
        part = lanes_of(g, g + 1)
        return pltpu.make_async_copy(x_hbm.at[:, part], xb.at[:, part], in_sem.at[g])

    v_copy = pltpu.make_async_copy(v_hbm, values, in_sem.at[groups])
    y_copy = pltpu.make_async_copy(y_hbm, yb, in_sem.at[groups + 1])
    small = [
        pltpu.make_async_copy(a, b, small_sem.at[i])
        for i, (a, b) in enumerate(
            (
                (count_hbm, count_ref),
                (rows_hbm, rows_ref),
                (cols_hbm, cols_ref),
                (coupling_hbm, coupling_ref),
            )
        )
    ]
    for g in range(groups):
        x_copy(g).start()
    barrier = pltpu.get_barrier_semaphore()

    def greet(d, carry):
        pl.semaphore_signal(
            barrier, inc=1, device_id=device(lax.rem(me + d, n)), device_id_type=MESH
        )
        return carry

    lax.fori_loop(1, n, greet, 0)

    for copy in small:
        copy.start()
    v_copy.start()
    y_copy.start()

    right = device(lax.rem(me + 1, n))
    left = device(lax.rem(me + n - 1, n))

    def halo_copy(step, side, g, h):
        win = wins[step]
        return pltpu.make_async_remote_copy(
            src_ref=win.at[g, pl.ds(cells + h * half, half)],
            dst_ref=win.at[g, pl.ds(2 * cells * side + h * half, half)],
            send_sem=send_sem.at[step, side, g, h],
            recv_sem=recv_sem.at[step, side, g, h],
            device_id=left if side else right,
            device_id_type=MESH,
        )

    def arrived(step, side, g, h):
        win = wins[step]
        pltpu.make_async_remote_copy(
            src_ref=win.at[g, pl.ds(cells + h * half, half)],
            dst_ref=win.at[g, pl.ds(2 * cells * side + h * half, half)],
            send_sem=send_sem.at[step, 0, g, h],
            recv_sem=recv_sem.at[step, side, g, h],
            device_id=right,
            device_id_type=MESH,
        ).wait_recv()

    for g in range(groups):
        x_copy(g).wait()
        win0[g, pl.ds(cells, cells), :] = xb[:, lanes_of(g, g + 1)].astype(BF16)
        if g == 0:
            pl.semaphore_wait(barrier, n - 1)
        for h in range(HALVES):
            for side in (0, 1):
                halo_copy(0, side, g, h).start()

    for copy in small:
        copy.wait()
    lanes = lax.broadcasted_iota(jnp.int32, (1, slots), 1)
    keys[...] = jnp.full(keys.shape, -1, jnp.int32)
    keys[:, :slots] = jnp.where(lanes < count_ref[0], rows_ref[...] * sources + cols_ref[...], -1)
    wide_s, wide_c = prev_v.shape[1], last_v.shape[1]
    first = lax.broadcasted_iota(jnp.int32, (wide_s, wide_s), 0)
    second = lax.broadcasted_iota(jnp.int32, (wide_s, wide_s), 1)
    key_row = keys[...]
    key_col = jnp.sum(jnp.where(first == second, key_row, 0), axis=1, keepdims=True)
    best = jnp.max(
        jnp.where((key_col == key_row) & (first < second), first, -1), axis=0, keepdims=True
    )
    prev_v[...] = jnp.where(best < 0, slots, best)
    slot = lax.broadcasted_iota(jnp.int32, (wide_s, wide_c), 0)
    cell = lax.broadcasted_iota(jnp.int32, (wide_s, wide_c), 1)
    best = jnp.max(jnp.where(key_col == cell, slot, -1), axis=0, keepdims=True)
    last_v[...] = jnp.where(best < 0, slots, best)
    prev_copy = pltpu.make_async_copy(prev_v, prev_ref, table_sem.at[0])
    last_copy = pltpu.make_async_copy(last_v, last_ref, table_sem.at[1])
    prev_copy.start()
    last_copy.start()

    group_r = group_index(lax.broadcasted_iota(jnp.int32, (width, width), 0), channels, replicas)
    group_c = group_index(lax.broadcasted_iota(jnp.int32, (width, width), 1), channels, replicas)
    same = group_r == group_c
    ones[...] = jnp.where(same, 1.0, 0.0).astype(BF16)
    pick_c = lax.broadcasted_iota(jnp.int32, (channels, width), 1)
    pick_c = pick_c - channels * group_index(pick_c, channels, replicas)
    pick = jnp.where(
        pick_c == lax.broadcasted_iota(jnp.int32, (channels, width), 0), 1.0, 0.0
    ).astype(BF16)
    pick_r = lax.broadcasted_iota(jnp.int32, (width, channels), 0)
    pick_r = pick_r - channels * group_index(pick_r, channels, replicas)
    pick_t = jnp.where(
        pick_r == lax.broadcasted_iota(jnp.int32, (width, channels), 1), 1.0, 0.0
    ).astype(BF16)
    wide = jnp.dot(coupling_ref[...], pick, preferred_element_type=F32).astype(BF16)
    full = jnp.dot(pick_t, wide, preferred_element_type=F32)
    mix[...] = jnp.where(same, full, 0.0).astype(BF16)

    sums[slots] = jnp.zeros((tile, tile), F32)
    v_copy.wait()
    prev_copy.wait()
    last_copy.wait()

    def add_tile(s, carry):
        sums[s] = sums[prev_ref[0, s]] + values[s].astype(F32)
        return carry

    lax.fori_loop(0, slots, add_tile, 0)

    def place(i, carry):
        p, t = lax.div(i, targets), lax.rem(i, targets)
        at = pl.ds(pl.multiple_of(t * tile, tile), tile)
        for j in range(targets):
            total = sums[last_ref[0, t * sources + p * targets + j]]
            high = total.astype(BF16)
            dense_hi[p, at, j * tile:(j + 1) * tile] = high
            dense_lo[p, at, j * tile:(j + 1) * tile] = (total - high.astype(F32)).astype(BF16)
        return carry

    lax.fori_loop(0, 3 * targets, place, 0)
    y_copy.wait()

    def product(step, block, first, last, start, size):
        rows = pl.ds(pl.multiple_of(block * cells + start, size), size)
        part = pl.ds(start, size)
        source = jnp.concatenate([wins[step][g, rows, :] for g in range(first, last)], axis=1)
        return jnp.dot(dense_hi[block, :, part], source, preferred_element_type=F32) + jnp.dot(
            dense_lo[block, :, part], source, preferred_element_type=F32
        )

    def needs(first, last):
        start = first * LANES // channels * channels // LANES
        stop = -(-min(-(-last * LANES // channels) * channels, width) // LANES)
        return start, stop

    def base(step, b):
        at = pl.ds(pl.multiple_of(b * half, half), half)
        x = xb[at, :]
        high = x.astype(BF16)
        low = (x - high.astype(F32)).astype(BF16)
        totals = jnp.dot(high, ones[...], preferred_element_type=F32) + jnp.dot(
            low, ones[...], preferred_element_type=F32
        )
        penalty = 0.02 * (totals - (2.0 - channels))
        detune = 1.0 - (step + 1.0) / (STEPS + 1.0)
        yb[at, :] = yb[at, :] + 0.5 * (-detune * x - 0.4 * penalty)

    def base_loop(b, carry):
        base(0, b)
        return carry

    lax.fori_loop(0, HALVES, base_loop, 0)

    near = 1 - lax.rem(col, 2)
    far = 1 - near
    per_half = chunks // HALVES

    def mixed_of(first, last, b):
        at = pl.ds(b * chunk, chunk)
        start, stop = needs(first, last)
        inner = lanes_of(start, stop)
        return jnp.dot(
            field[at, inner].astype(BF16), mix[inner, lanes_of(first, last)],
            preferred_element_type=F32,
        )

    def update(first, last, b, mixed):
        at = pl.ds(b * chunk, chunk)
        out = lanes_of(first, last)
        y = yb[at, out] - 0.2 * mixed
        x = jnp.clip(xb[at, out] + 0.5 * y, -1.0, 1.0)
        yb[at, out] = y
        xb[at, out] = x
        return x

    def add_energy(step, first, last, b, mixed):
        own_rows = pl.ds(cells + b * chunk, chunk)
        rounded = jnp.concatenate([wins[step][g, own_rows, :] for g in range(first, last)], axis=1)
        product_sum = (rounded.astype(F32) * mixed).reshape(chunk // 8, 8, mixed.shape[1])
        epart[:, lanes_of(first, last)] += jnp.sum(product_sum, axis=0)

    epart[...] = jnp.zeros(epart.shape, F32)
    late = None
    for step in range(STEPS):
        field[...] = product(step, 1, 0, groups, 0, cells)
        for g in range(groups):
            for h in range(HALVES):
                arrived(step, near, g, h)
        field[...] += product(step, 2 * near, 0, groups, 0, cells)
        done = 0
        for g in range(groups):
            for h in range(HALVES):
                arrived(step, far, g, h)
                field[:, lanes_of(g, g + 1)] += product(step, 2 * far, g, g + 1, h * half, half)
            ready = done
            while ready < groups and needs(ready, ready + 1)[1] <= g + 1:
                ready += 1
            if ready == done:
                continue
            for b in range(chunks):
                mixed = mixed_of(done, ready, b)
                if step == STEPS - 1:
                    add_energy(step, done, ready, b, mixed)
                    if ready == groups:
                        late = done
                        mixed_ref[pl.ds(b * chunk, chunk), lanes_of(done, ready)] = mixed
                    else:
                        update(done, ready, b, mixed)
                    continue
                x = update(done, ready, b, mixed)
                for send in range(done, ready):
                    wins[step + 1][send, pl.ds(cells + b * chunk, chunk), :] = x[
                        :, (send - done) * LANES:(send - done + 1) * LANES
                    ].astype(BF16)
                if (b + 1) % per_half == 0:
                    for send in range(done, ready):
                        for side in (0, 1):
                            halo_copy(step + 1, side, send, b // per_half).start()
            done = ready
        if step < STEPS - 1:
            for b in range(HALVES):
                base(step + 1, b)

    lane_sum = jnp.sum(epart[...], axis=0, keepdims=True)
    shape = (replicas, width)
    group = group_index(lax.broadcasted_iota(jnp.int32, shape, 1), channels, replicas)
    which = lax.broadcasted_iota(jnp.int32, shape, 0)
    share = jnp.sum(jnp.where(group == which, lane_sum, 0.0), axis=1, keepdims=True)
    shape = (replicas, 128)
    lane = lax.broadcasted_iota(jnp.int32, shape, 1)
    which = lax.broadcasted_iota(jnp.int32, shape, 0)
    eall[0] = jnp.sum(jnp.where(lane == which, share, 0.0), axis=0, keepdims=True)

    def energy_copy(d):
        return pltpu.make_async_remote_copy(
            src_ref=eall.at[0],
            dst_ref=eall.at[d],
            send_sem=esend_sem.at[d],
            recv_sem=erecv_sem.at[d],
            device_id=device(lax.rem(me + d, n)),
            device_id_type=MESH,
        )

    def send_energy(d, carry):
        energy_copy(d).start()
        return carry

    lax.fori_loop(1, n, send_energy, 0)
    for b in range(chunks):
        update(late, groups, b, mixed_ref[pl.ds(b * chunk, chunk), lanes_of(late, groups)])
    for step in range(STEPS):
        for side in (0, 1):
            for g in range(groups):
                for h in range(HALVES):
                    halo_copy(step, side, g, h).wait_send()

    def take_energy(d, carry):
        energy_copy(d).wait()
        return carry

    lax.fori_loop(1, n, take_energy, 0)
    e_out[...] = (jnp.sum(eall[...], axis=0) * scale)[:, :replicas]


def write_kernel(x_in, y_in, e_in, x_out, y_out, e_out, sem):
    x_copy = pltpu.make_async_copy(x_in, x_out, sem.at[0])
    y_copy = pltpu.make_async_copy(y_in, y_out, sem.at[1])
    x_copy.start()
    y_copy.start()
    e_copy = pltpu.make_async_copy(e_in, e_out, sem.at[2])
    e_copy.start()
    x_copy.wait()
    y_copy.wait()
    e_copy.wait()


def local(rows_n, cols_n, positions, momenta, tile_values, tile_rows, tile_cols, tile_count, channel_coupling):
    cells, width = positions.shape
    slots, tile, _ = tile_values.shape
    channels = channel_coupling.shape[0]
    replicas = width // channels
    targets = cells // tile
    wide_s = pl.cdiv(slots, 128) * 128
    wide_c = pl.cdiv(3 * targets * targets, 128) * 128
    groups = width // LANES
    n = rows_n * cols_n
    vmem = pl.BlockSpec(memory_space=pltpu.VMEM)
    hbm = pl.BlockSpec(memory_space=pltpu.HBM)
    anywhere = pl.BlockSpec(memory_space=pl.ANY)
    scale = 1.0 / float(cells * n * channels) ** 0.5
    x, y, e = pl.pallas_call(
        functools.partial(main_kernel, rows_n, cols_n, channels, scale),
        out_shape=(
            jax.ShapeDtypeStruct((cells, width), F32),
            jax.ShapeDtypeStruct((cells, width), F32),
            jax.ShapeDtypeStruct((1, replicas), F32),
        ),
        in_specs=[hbm] + [hbm] * 6,
        out_specs=(vmem, vmem, vmem),
        scratch_shapes=[
            pltpu.VMEM((groups, 3 * cells, LANES), BF16),
            pltpu.VMEM((groups, 3 * cells, LANES), BF16),
            pltpu.VMEM((slots, tile, tile), BF16),
            pltpu.VMEM((slots + 1, tile, tile), F32),
            pltpu.VMEM((3, cells, cells), BF16),
            pltpu.VMEM((3, cells, cells), BF16),
            pltpu.VMEM((cells, width), F32),
            pltpu.VMEM((cells, width), F32),
            pltpu.VMEM((width, width), BF16),
            pltpu.VMEM((width, width), BF16),
            pltpu.VMEM((8, width), F32),
            pltpu.VMEM((n, 1, 128), F32),
            pltpu.SMEM((1,), jnp.int32),
            pltpu.VMEM((1, slots), jnp.int32),
            pltpu.VMEM((1, slots), jnp.int32),
            pltpu.VMEM((channels, channels), BF16),
            pltpu.VMEM((1, wide_s), jnp.int32),
            pltpu.VMEM((1, wide_s), jnp.int32),
            pltpu.VMEM((1, wide_c), jnp.int32),
            pltpu.SMEM((1, wide_s), jnp.int32),
            pltpu.SMEM((1, wide_c), jnp.int32),
            pltpu.SemaphoreType.DMA((groups + 2,)),
            pltpu.SemaphoreType.DMA((4,)),
            pltpu.SemaphoreType.DMA((2,)),
            pltpu.SemaphoreType.DMA((STEPS, 2, groups, HALVES)),
            pltpu.SemaphoreType.DMA((STEPS, 2, groups, HALVES)),
            pltpu.SemaphoreType.DMA((n,)),
            pltpu.SemaphoreType.DMA((n,)),
        ],
        compiler_params=pltpu.CompilerParams(
            collective_id=0, has_side_effects=True, vmem_limit_bytes=42 << 20
        ),
        name="steps",
    )(
        tile_count,
        *(
            pltpu.with_memory_space_constraint(a, pltpu.HBM)
            for a in (
                tile_rows.reshape(1, slots), tile_cols.reshape(1, slots),
                channel_coupling, positions, momenta, tile_values,
            )
        )
    )
    x, y, e = pl.pallas_call(
        write_kernel,
        out_shape=(
            jax.ShapeDtypeStruct((cells, width), F32),
            jax.ShapeDtypeStruct((cells, width), F32),
            jax.ShapeDtypeStruct((1, replicas), F32),
        ),
        in_specs=[anywhere, anywhere, anywhere],
        out_specs=(hbm, hbm, hbm),
        scratch_shapes=[pltpu.SemaphoreType.DMA((3,))],
        compiler_params=pltpu.CompilerParams(vmem_limit_bytes=1 << 20),
        name="write",
    )(x, y, e)
    return x, y, e.reshape(replicas)


def solution(mesh):
    return jax.shard_map(
        functools.partial(local, mesh.shape["row"], mesh.shape["col"]),
        mesh=mesh,
        in_specs=(
            P(("groups", "row", "col"), None),
            P(("groups", "row", "col"), None),
            P(("groups", "row", "col"), None, None),
            P(("groups", "row", "col")),
            P(("groups", "row", "col")),
            P(("groups", "row", "col")),
            P(),
        ),
        out_specs=(
            P(("groups", "row", "col"), None),
            P(("groups", "row", "col"), None),
            P("groups"),
        ),
        check_vma=False,
    )
```

```python
import functools

import jax
import jax.numpy as jnp
from jax import lax
from jax.experimental import pallas as pl
from jax.experimental.pallas import tpu as pltpu
from jax.sharding import PartitionSpec as P

STEPS = 2
LANES = 128
HALVES = 2
MESH = pl.DeviceIdType.MESH
F32 = jnp.float32
BF16 = jnp.bfloat16
F8 = jnp.float8_e4m3fn
LOW_SCALE = 4096.0


def group_index(index, channels, replicas):
    group = jnp.zeros(index.shape, jnp.int32)
    for r in range(1, replicas):
        group = group + (index >= r * channels).astype(jnp.int32)
    return group


def main_kernel(
    rows_n, cols_n, channels, scale,
    count_hbm, rows_hbm, cols_hbm, coupling_hbm, x_hbm, y_hbm, v_hbm,
    xb, yb, e_out,
    win0, win1, values, sums, dense_hi, dense_lo, field, mixed_ref, mix, ones, epart, eall,
    count_ref, rows_ref, cols_ref, coupling_ref, keys, prev_v, last_v, prev_ref, last_ref,
    in_sem, small_sem, table_sem, gate_sem, send_sem, recv_sem, esend_sem, erecv_sem,
):
    cells, width = xb.shape
    slots, tile, _ = values.shape
    chunk = 2 * tile
    chunks = cells // chunk
    targets = cells // tile
    sources = 3 * targets
    replicas = width // channels
    groups = width // LANES
    half = cells // HALVES
    n = rows_n * cols_n
    wins = (win0, win1)
    row, col = lax.axis_index("row"), lax.axis_index("col")
    me = row * cols_n + col

    def device(flat):
        return {"row": lax.div(flat, cols_n), "col": lax.rem(flat, cols_n)}

    def lanes_of(first, last):
        return pl.ds(first * LANES, (last - first) * LANES)

    def x_copy(g):
        part = lanes_of(g, g + 1)
        return pltpu.make_async_copy(x_hbm.at[:, part], xb.at[:, part], in_sem.at[g])

    v_copy = pltpu.make_async_copy(v_hbm, values, in_sem.at[groups])
    y_copy = pltpu.make_async_copy(y_hbm, yb, in_sem.at[groups + 1])
    small = [
        pltpu.make_async_copy(a, b, small_sem.at[i])
        for i, (a, b) in enumerate(
            (
                (count_hbm, count_ref),
                (rows_hbm, rows_ref),
                (cols_hbm, cols_ref),
                (coupling_hbm, coupling_ref),
            )
        )
    ]
    for g in range(groups):
        x_copy(g).start()
    barrier = pltpu.get_barrier_semaphore()

    def greet(d):
        pl.semaphore_signal(
            barrier, inc=1, device_id=device(lax.rem(me + d, n)), device_id_type=MESH
        )

    def greet_both(d, carry):
        greet(d)
        greet(n - d)
        return carry

    lax.fori_loop(1, n // 2, greet_both, 0)
    greet(n // 2)

    for copy in small:
        copy.start()
    y_copy.start()
    v_copy.start()

    right = device(lax.rem(me + 1, n))
    left = device(lax.rem(me + n - 1, n))

    def halo_copy(step, side, g, h):
        win = wins[step]
        return pltpu.make_async_remote_copy(
            src_ref=win.at[g, pl.ds(cells + h * half, half)],
            dst_ref=win.at[g, pl.ds(2 * cells * side + h * half, half)],
            send_sem=send_sem.at[step, side, g, h],
            recv_sem=recv_sem.at[step, side, g, h],
            device_id=left if side else right,
            device_id_type=MESH,
        )

    def arrived(step, side, g, h):
        win = wins[step]
        pltpu.make_async_remote_copy(
            src_ref=win.at[g, pl.ds(cells + h * half, half)],
            dst_ref=win.at[g, pl.ds(2 * cells * side + h * half, half)],
            send_sem=send_sem.at[step, 0, g, h],
            recv_sem=recv_sem.at[step, side, g, h],
            device_id=right,
            device_id_type=MESH,
        ).wait_recv()

    for g in range(groups):
        x_copy(g).wait()
        win0[g, pl.ds(cells, cells), :] = xb[:, lanes_of(g, g + 1)].astype(BF16)
        if g == 0:
            pl.semaphore_wait(barrier, n - 1)
        for h in range(HALVES):
            for side in (0, 1):
                halo_copy(0, side, g, h).start()

    for copy in small:
        copy.wait()
    lanes = lax.broadcasted_iota(jnp.int32, (1, slots), 1)
    keys[...] = jnp.full(keys.shape, -1, jnp.int32)
    keys[:, :slots] = jnp.where(lanes < count_ref[0], rows_ref[...] * sources + cols_ref[...], -1)
    wide_s, wide_c = prev_v.shape[1], last_v.shape[1]
    first = lax.broadcasted_iota(jnp.int32, (wide_s, wide_s), 0)
    second = lax.broadcasted_iota(jnp.int32, (wide_s, wide_s), 1)
    key_row = keys[...]
    key_col = jnp.sum(jnp.where(first == second, key_row, 0), axis=1, keepdims=True)
    best = jnp.max(
        jnp.where((key_col == key_row) & (first < second), first, -1), axis=0, keepdims=True
    )
    prev_v[...] = jnp.where(best < 0, slots, best)
    slot = lax.broadcasted_iota(jnp.int32, (wide_s, wide_c), 0)
    cell = lax.broadcasted_iota(jnp.int32, (wide_s, wide_c), 1)
    best = jnp.max(jnp.where(key_col == cell, slot, -1), axis=0, keepdims=True)
    last_v[...] = jnp.where(best < 0, slots, best)
    prev_copy = pltpu.make_async_copy(prev_v, prev_ref, table_sem.at[0])
    last_copy = pltpu.make_async_copy(last_v, last_ref, table_sem.at[1])
    prev_copy.start()
    last_copy.start()

    group_r = group_index(lax.broadcasted_iota(jnp.int32, (width, width), 0), channels, replicas)
    group_c = group_index(lax.broadcasted_iota(jnp.int32, (width, width), 1), channels, replicas)
    same = group_r == group_c
    ones[...] = jnp.where(same, 1.0, 0.0).astype(BF16)
    pick_c = lax.broadcasted_iota(jnp.int32, (channels, width), 1)
    pick_c = pick_c - channels * group_index(pick_c, channels, replicas)
    pick = jnp.where(
        pick_c == lax.broadcasted_iota(jnp.int32, (channels, width), 0), 1.0, 0.0
    ).astype(BF16)
    pick_r = lax.broadcasted_iota(jnp.int32, (width, channels), 0)
    pick_r = pick_r - channels * group_index(pick_r, channels, replicas)
    pick_t = jnp.where(
        pick_r == lax.broadcasted_iota(jnp.int32, (width, channels), 1), 1.0, 0.0
    ).astype(BF16)
    wide = jnp.dot(coupling_ref[...], pick, preferred_element_type=F32).astype(BF16)
    full = jnp.dot(pick_t, wide, preferred_element_type=F32)
    mix[...] = jnp.where(same, full, 0.0).astype(BF16)

    def base(step, b):
        at = pl.ds(pl.multiple_of(b * half, half), half)
        x = xb[at, :]
        high = x.astype(BF16)
        low = (x - high.astype(F32)).astype(BF16)
        totals = jnp.dot(high, ones[...], preferred_element_type=F32) + jnp.dot(
            low, ones[...], preferred_element_type=F32
        )
        penalty = 0.02 * (totals - (2.0 - channels))
        detune = 1.0 - (step + 1.0) / (STEPS + 1.0)
        yb[at, :] = yb[at, :] + 0.5 * (-detune * x - 0.4 * penalty)

    def base_loop(b, carry):
        base(0, b)
        return carry

    y_copy.wait()
    lax.fori_loop(0, HALVES, base_loop, 0)
    sums[slots] = jnp.zeros((tile, tile), F32)
    v_copy.wait()
    prev_copy.wait()
    last_copy.wait()

    def add_tile(s, carry):
        sums[s] = sums[prev_ref[0, s]] + values[s].astype(F32)
        return carry

    lax.fori_loop(0, slots, add_tile, 0, unroll=4)

    def place(i, carry):
        p, t = lax.div(i, targets), lax.rem(i, targets)
        at = pl.ds(pl.multiple_of(t * tile, tile), tile)
        for j in range(targets):
            total = sums[last_ref[0, t * sources + p * targets + j]]
            high = total.astype(BF16)
            dense_hi[p, at, j * tile:(j + 1) * tile] = high
            low = (total - high.astype(F32)) * LOW_SCALE
            dense_lo[p, at, j * tile:(j + 1) * tile] = low.astype(F8)
        return carry

    lax.fori_loop(0, 3 * targets, place, 0)

    def product(step, block, first, last, start, size):
        rows = pl.ds(pl.multiple_of(block * cells + start, size), size)
        part = pl.ds(start, size)
        source = jnp.concatenate([wins[step][g, rows, :] for g in range(first, last)], axis=1)
        low = jnp.dot(dense_lo[block, :, part], source.astype(F8), preferred_element_type=F32)
        high = jnp.dot(dense_hi[block, :, part], source, preferred_element_type=F32)
        return high + low * (1.0 / LOW_SCALE)

    def needs(first, last):
        start = first * LANES // channels * channels // LANES
        stop = -(-min(-(-last * LANES // channels) * channels, width) // LANES)
        return start, stop

    near = 1 - lax.rem(col, 2)
    far = 1 - near
    per_half = chunks // HALVES

    def mixed_of(first, last, b):
        at = pl.ds(b * chunk, chunk)
        start, stop = needs(first, last)
        inner = lanes_of(start, stop)
        return jnp.dot(
            field[at, inner].astype(BF16), mix[inner, lanes_of(first, last)],
            preferred_element_type=F32,
        )

    def update(first, last, b, mixed):
        at = pl.ds(b * chunk, chunk)
        out = lanes_of(first, last)
        y = yb[at, out] - 0.2 * mixed
        x = jnp.clip(xb[at, out] + 0.5 * y, -1.0, 1.0)
        yb[at, out] = y
        xb[at, out] = x
        return x

    def add_energy(step, first, last, b, mixed):
        own_rows = pl.ds(cells + b * chunk, chunk)
        rounded = jnp.concatenate([wins[step][g, own_rows, :] for g in range(first, last)], axis=1)
        product_sum = (rounded.astype(F32) * mixed).reshape(chunk // 8, 8, mixed.shape[1])
        epart[:, lanes_of(first, last)] += jnp.sum(product_sum, axis=0)

    epart[...] = jnp.zeros(epart.shape, F32)
    late = None
    for step in range(STEPS):
        field[...] = product(step, 1, 0, groups, 0, cells)
        for g in range(groups):
            for h in range(HALVES):
                arrived(step, near, g, h)
        field[...] += product(step, 2 * near, 0, groups, 0, cells)
        done = 0
        for g in range(groups):
            for h in range(HALVES):
                arrived(step, far, g, h)
                if step < STEPS - 1 and (g, h) == (2, 0):
                    @pl.when(lax.rem(row, 2) != lax.rem(col, 2))
                    def _():
                        pl.semaphore_signal(gate_sem, inc=1, device_id=device(me + 1 - 2 * lax.rem(col, 2)), device_id_type=MESH)
                field[:, lanes_of(g, g + 1)] += product(step, 2 * far, g, g + 1, h * half, half)
            ready = done
            while ready < groups and needs(ready, ready + 1)[1] <= g + 1:
                ready += 1
            if ready == done:
                continue
            if step < STEPS - 1 and done == 0:
                @pl.when(lax.rem(row, 2) == lax.rem(col, 2))
                def _():
                    pl.semaphore_wait(gate_sem, 1)
            for b in range(chunks):
                mixed = mixed_of(done, ready, b)
                if step == STEPS - 1:
                    add_energy(step, done, ready, b, mixed)
                    if ready == groups:
                        late = done
                        mixed_ref[pl.ds(b * chunk, chunk), lanes_of(done, ready)] = mixed
                    else:
                        update(done, ready, b, mixed)
                    continue
                x = update(done, ready, b, mixed)
                for send in range(done, ready):
                    wins[step + 1][send, pl.ds(cells + b * chunk, chunk), :] = x[
                        :, (send - done) * LANES:(send - done + 1) * LANES
                    ].astype(BF16)
                if (b + 1) % per_half == 0:
                    for send in range(done, ready):
                        for side in (0, 1):
                            halo_copy(step + 1, side, send, b // per_half).start()
            done = ready
        if step < STEPS - 1:
            for b in range(HALVES):
                base(step + 1, b)

    lane_sum = jnp.sum(epart[...], axis=0, keepdims=True)
    shape = (replicas, width)
    group = group_index(lax.broadcasted_iota(jnp.int32, shape, 1), channels, replicas)
    which = lax.broadcasted_iota(jnp.int32, shape, 0)
    share = jnp.sum(jnp.where(group == which, lane_sum, 0.0), axis=1, keepdims=True)
    shape = (replicas, 128)
    lane = lax.broadcasted_iota(jnp.int32, shape, 1)
    which = lax.broadcasted_iota(jnp.int32, shape, 0)
    eall[0] = jnp.sum(jnp.where(lane == which, share, 0.0), axis=0, keepdims=True)

    def energy_copy(d):
        return pltpu.make_async_remote_copy(
            src_ref=eall.at[0],
            dst_ref=eall.at[d],
            send_sem=esend_sem.at[d],
            recv_sem=erecv_sem.at[d],
            device_id=device(lax.rem(me + d, n)),
            device_id_type=MESH,
        )

    def send_energy(d, carry):
        energy_copy(d).start()
        return carry

    lax.fori_loop(1, n, send_energy, 0)
    for b in range(chunks):
        update(late, groups, b, mixed_ref[pl.ds(b * chunk, chunk), lanes_of(late, groups)])
    for step in range(STEPS):
        for side in (0, 1):
            for g in range(groups):
                for h in range(HALVES):
                    halo_copy(step, side, g, h).wait_send()

    def take_energy(d, carry):
        energy_copy(d).wait()
        return carry

    lax.fori_loop(1, n, take_energy, 0)
    e_out[...] = (jnp.sum(eall[...], axis=0) * scale)[:, :replicas]


def write_kernel(x_in, y_in, e_in, x_out, y_out, e_out, sem):
    x_copy = pltpu.make_async_copy(x_in, x_out, sem.at[0])
    y_copy = pltpu.make_async_copy(y_in, y_out, sem.at[1])
    x_copy.start()
    y_copy.start()
    e_copy = pltpu.make_async_copy(e_in, e_out, sem.at[2])
    e_copy.start()
    x_copy.wait()
    y_copy.wait()
    e_copy.wait()


def local(rows_n, cols_n, positions, momenta, tile_values, tile_rows, tile_cols, tile_count, channel_coupling):
    cells, width = positions.shape
    slots, tile, _ = tile_values.shape
    channels = channel_coupling.shape[0]
    replicas = width // channels
    targets = cells // tile
    wide_s = pl.cdiv(slots, 128) * 128
    wide_c = pl.cdiv(3 * targets * targets, 128) * 128
    groups = width // LANES
    n = rows_n * cols_n
    vmem = pl.BlockSpec(memory_space=pltpu.VMEM)
    hbm = pl.BlockSpec(memory_space=pltpu.HBM)
    anywhere = pl.BlockSpec(memory_space=pl.ANY)
    scale = 1.0 / float(cells * n * channels) ** 0.5
    x, y, e = pl.pallas_call(
        functools.partial(main_kernel, rows_n, cols_n, channels, scale),
        out_shape=(
            jax.ShapeDtypeStruct((cells, width), F32),
            jax.ShapeDtypeStruct((cells, width), F32),
            jax.ShapeDtypeStruct((1, replicas), F32),
        ),
        in_specs=[hbm] + [hbm] * 6,
        out_specs=(vmem, vmem, vmem),
        scratch_shapes=[
            pltpu.VMEM((groups, 3 * cells, LANES), BF16),
            pltpu.VMEM((groups, 3 * cells, LANES), BF16),
            pltpu.VMEM((slots, tile, tile), BF16),
            pltpu.VMEM((slots + 1, tile, tile), F32),
            pltpu.VMEM((3, cells, cells), BF16),
            pltpu.VMEM((3, cells, cells), F8),
            pltpu.VMEM((cells, width), F32),
            pltpu.VMEM((cells, width), F32),
            pltpu.VMEM((width, width), BF16),
            pltpu.VMEM((width, width), BF16),
            pltpu.VMEM((8, width), F32),
            pltpu.VMEM((n, 1, 128), F32),
            pltpu.SMEM((1,), jnp.int32),
            pltpu.VMEM((1, slots), jnp.int32),
            pltpu.VMEM((1, slots), jnp.int32),
            pltpu.VMEM((channels, channels), BF16),
            pltpu.VMEM((1, wide_s), jnp.int32),
            pltpu.VMEM((1, wide_s), jnp.int32),
            pltpu.VMEM((1, wide_c), jnp.int32),
            pltpu.SMEM((1, wide_s), jnp.int32),
            pltpu.SMEM((1, wide_c), jnp.int32),
            pltpu.SemaphoreType.DMA((groups + 2,)),
            pltpu.SemaphoreType.DMA((4,)),
            pltpu.SemaphoreType.DMA((2,)),
            pltpu.SemaphoreType.REGULAR,
            pltpu.SemaphoreType.DMA((STEPS, 2, groups, HALVES)),
            pltpu.SemaphoreType.DMA((STEPS, 2, groups, HALVES)),
            pltpu.SemaphoreType.DMA((n,)),
            pltpu.SemaphoreType.DMA((n,)),
        ],
        compiler_params=pltpu.CompilerParams(
            collective_id=0, has_side_effects=True, vmem_limit_bytes=42 << 20
        ),
        name="steps",
    )(
        tile_count,
        *(
            pltpu.with_memory_space_constraint(a, pltpu.HBM)
            for a in (
                tile_rows.reshape(1, slots), tile_cols.reshape(1, slots),
                channel_coupling, positions, momenta, tile_values,
            )
        )
    )
    x, y, e = pl.pallas_call(
        write_kernel,
        out_shape=(
            jax.ShapeDtypeStruct((cells, width), F32),
            jax.ShapeDtypeStruct((cells, width), F32),
            jax.ShapeDtypeStruct((1, replicas), F32),
        ),
        in_specs=[anywhere, anywhere, anywhere],
        out_specs=(hbm, hbm, hbm),
        scratch_shapes=[pltpu.SemaphoreType.DMA((3,))],
        compiler_params=pltpu.CompilerParams(vmem_limit_bytes=1 << 20),
        name="write",
    )(x, y, e)
    return x, y, e.reshape(replicas)


def solution(mesh):
    return jax.shard_map(
        functools.partial(local, mesh.shape["row"], mesh.shape["col"]),
        mesh=mesh,
        in_specs=(
            P(("groups", "row", "col"), None),
            P(("groups", "row", "col"), None),
            P(("groups", "row", "col"), None, None),
            P(("groups", "row", "col")),
            P(("groups", "row", "col")),
            P(("groups", "row", "col")),
            P(),
        ),
        out_specs=(
            P(("groups", "row", "col"), None),
            P(("groups", "row", "col"), None),
            P("groups"),
        ),
        check_vma=False,
    )
```

```python
import functools

import jax
import jax.numpy as jnp
from jax import lax
from jax.experimental import pallas as pl
from jax.experimental.pallas import tpu as pltpu
from jax.sharding import PartitionSpec as P

STEPS = 2
LANES = 128
HALVES = 2
MESH = pl.DeviceIdType.MESH
F32 = jnp.float32
BF16 = jnp.bfloat16
F8 = jnp.float8_e4m3fn
LOW_SCALE = 4096.0


def group_index(index, channels, replicas):
    group = jnp.zeros(index.shape, jnp.int32)
    for r in range(1, replicas):
        group = group + (index >= r * channels).astype(jnp.int32)
    return group


def main_kernel(
    rows_n, cols_n, channels, scale,
    count_hbm, rows_hbm, cols_hbm, coupling_hbm, x_hbm, y_hbm, v_hbm,
    xb, yb, e_out,
    win0, win1, values, sums, dense_hi, dense_lo, field, mixed_ref, mix, ones, epart, eall,
    count_ref, rows_ref, cols_ref, coupling_ref, keys, prev_v, last_v, prev_ref, last_ref,
    in_sem, small_sem, table_sem, gate_sem, known_sem, send_sem, recv_sem, esend_sem, erecv_sem,
):
    cells, width = xb.shape
    slots, tile, _ = values.shape
    chunk = 4 * tile
    chunks = cells // chunk
    targets = cells // tile
    sources = 3 * targets
    replicas = width // channels
    groups = width // LANES
    half = cells // HALVES
    n = rows_n * cols_n
    wins = (win0, win1)
    row, col = lax.axis_index("row"), lax.axis_index("col")
    me = row * cols_n + col

    def device(flat):
        return {"row": lax.div(flat, cols_n), "col": lax.rem(flat, cols_n)}

    def lanes_of(first, last):
        return pl.ds(first * LANES, (last - first) * LANES)

    def x_copy(g):
        part = lanes_of(g, g + 1)
        return pltpu.make_async_copy(x_hbm.at[:, part], xb.at[:, part], in_sem.at[g])

    v_copy = pltpu.make_async_copy(v_hbm, values, in_sem.at[groups])
    y_copy = pltpu.make_async_copy(y_hbm, yb, in_sem.at[groups + 1])
    small = [
        pltpu.make_async_copy(a, b, small_sem.at[i])
        for i, (a, b) in enumerate(
            (
                (count_hbm, count_ref),
                (rows_hbm, rows_ref),
                (cols_hbm, cols_ref),
                (coupling_hbm, coupling_ref),
            )
        )
    ]
    for g in range(groups):
        x_copy(g).start()
    barrier = pltpu.get_barrier_semaphore()

    def tell(sem, d):
        pl.semaphore_signal(
            sem, inc=1, device_id=device(lax.rem(me + n + d, n)), device_id_type=MESH
        )

    tell(barrier, 1)
    tell(barrier, -1)
    rounds = known_sem.shape[0]
    passed = [0]

    def spread():
        k = passed[0]
        if 0 < k <= rounds:
            for side in (0, 1):
                pl.semaphore_wait(known_sem.at[k - 1, side], 1)
        if k < rounds:
            tell(known_sem.at[k, 0], 1 << k)
            tell(known_sem.at[k, 1], -(1 << k))
        passed[0] = k + 1

    for copy in small:
        copy.start()
    y_copy.start()
    v_copy.start()

    right = device(lax.rem(me + 1, n))
    left = device(lax.rem(me + n - 1, n))

    def halo_copy(step, side, g, h):
        win = wins[step]
        return pltpu.make_async_remote_copy(
            src_ref=win.at[g, pl.ds(cells + h * half, half)],
            dst_ref=win.at[g, pl.ds(2 * cells * side + h * half, half)],
            send_sem=send_sem.at[step, side, g, h],
            recv_sem=recv_sem.at[step, side, g, h],
            device_id=left if side else right,
            device_id_type=MESH,
        )

    def arrived(step, side, g, h):
        win = wins[step]
        pltpu.make_async_remote_copy(
            src_ref=win.at[g, pl.ds(cells + h * half, half)],
            dst_ref=win.at[g, pl.ds(2 * cells * side + h * half, half)],
            send_sem=send_sem.at[step, 0, g, h],
            recv_sem=recv_sem.at[step, side, g, h],
            device_id=right,
            device_id_type=MESH,
        ).wait_recv()

    for g in range(groups):
        x_copy(g).wait()
        win0[g, pl.ds(cells, cells), :] = xb[:, lanes_of(g, g + 1)].astype(BF16)
        if g == 0:
            pl.semaphore_wait(barrier, 2)
        for h in range(HALVES):
            for side in (0, 1):
                halo_copy(0, side, g, h).start()

    spread()
    for copy in small:
        copy.wait()
    lanes = lax.broadcasted_iota(jnp.int32, (1, slots), 1)
    keys[...] = jnp.full(keys.shape, -1, jnp.int32)
    keys[:, :slots] = jnp.where(lanes < count_ref[0], rows_ref[...] * sources + cols_ref[...], -1)
    wide_s, wide_c = prev_v.shape[1], last_v.shape[1]
    first = lax.broadcasted_iota(jnp.int32, (wide_s, wide_s), 0)
    second = lax.broadcasted_iota(jnp.int32, (wide_s, wide_s), 1)
    key_row = keys[...]
    key_col = jnp.sum(jnp.where(first == second, key_row, 0), axis=1, keepdims=True)
    best = jnp.max(
        jnp.where((key_col == key_row) & (first < second), first, -1), axis=0, keepdims=True
    )
    prev_v[...] = jnp.where(best < 0, slots, best)
    slot = lax.broadcasted_iota(jnp.int32, (wide_s, wide_c), 0)
    cell = lax.broadcasted_iota(jnp.int32, (wide_s, wide_c), 1)
    best = jnp.max(jnp.where(key_col == cell, slot, -1), axis=0, keepdims=True)
    last_v[...] = jnp.where(best < 0, slots, best)
    prev_copy = pltpu.make_async_copy(prev_v, prev_ref, table_sem.at[0])
    last_copy = pltpu.make_async_copy(last_v, last_ref, table_sem.at[1])
    prev_copy.start()
    last_copy.start()

    group_r = group_index(lax.broadcasted_iota(jnp.int32, (width, width), 0), channels, replicas)
    group_c = group_index(lax.broadcasted_iota(jnp.int32, (width, width), 1), channels, replicas)
    same = group_r == group_c
    ones[...] = jnp.where(same, 1.0, 0.0).astype(BF16)
    pick_c = lax.broadcasted_iota(jnp.int32, (channels, width), 1)
    pick_c = pick_c - channels * group_index(pick_c, channels, replicas)
    pick = jnp.where(
        pick_c == lax.broadcasted_iota(jnp.int32, (channels, width), 0), 1.0, 0.0
    ).astype(BF16)
    pick_r = lax.broadcasted_iota(jnp.int32, (width, channels), 0)
    pick_r = pick_r - channels * group_index(pick_r, channels, replicas)
    pick_t = jnp.where(
        pick_r == lax.broadcasted_iota(jnp.int32, (width, channels), 1), 1.0, 0.0
    ).astype(BF16)
    wide = jnp.dot(coupling_ref[...], pick, preferred_element_type=F32).astype(BF16)
    full = jnp.dot(pick_t, wide, preferred_element_type=F32)
    mix[...] = jnp.where(same, full, 0.0).astype(BF16)

    def base(step, b):
        at = pl.ds(pl.multiple_of(b * half, half), half)
        x = xb[at, :]
        high = x.astype(BF16)
        low = (x - high.astype(F32)).astype(BF16)
        totals = jnp.dot(high, ones[...], preferred_element_type=F32) + jnp.dot(
            low, ones[...], preferred_element_type=F32
        )
        penalty = 0.02 * (totals - (2.0 - channels))
        detune = 1.0 - (step + 1.0) / (STEPS + 1.0)
        yb[at, :] = yb[at, :] + 0.5 * (-detune * x - 0.4 * penalty)

    def base_loop(b, carry):
        base(0, b)
        return carry

    y_copy.wait()
    lax.fori_loop(0, HALVES, base_loop, 0)
    sums[slots] = jnp.zeros((tile, tile), F32)
    v_copy.wait()
    prev_copy.wait()
    last_copy.wait()

    def add_tile(s, carry):
        sums[s] = sums[prev_ref[0, s]] + values[s].astype(F32)
        return carry

    lax.fori_loop(0, slots, add_tile, 0, unroll=4)

    def place(i, carry):
        p, t = lax.div(i, targets), lax.rem(i, targets)
        at = pl.ds(pl.multiple_of(t * tile, tile), tile)
        for j in range(targets):
            total = sums[last_ref[0, t * sources + p * targets + j]]
            high = total.astype(BF16)
            dense_hi[p, at, j * tile:(j + 1) * tile] = high
            low = (total - high.astype(F32)) * LOW_SCALE
            dense_lo[p, at, j * tile:(j + 1) * tile] = low.astype(F8)
        return carry

    lax.fori_loop(0, 3 * targets, place, 0)
    spread()

    def product(step, block, first, last, start, size):
        rows = pl.ds(pl.multiple_of(block * cells + start, size), size)
        part = pl.ds(start, size)
        source = jnp.concatenate([wins[step][g, rows, :] for g in range(first, last)], axis=1)
        low = jnp.dot(dense_lo[block, :, part], source.astype(F8), preferred_element_type=F32)
        high = jnp.dot(dense_hi[block, :, part], source, preferred_element_type=F32)
        return high + low * (1.0 / LOW_SCALE)

    def needs(first, last):
        start = first * LANES // channels * channels // LANES
        stop = -(-min(-(-last * LANES // channels) * channels, width) // LANES)
        return start, stop

    near = 1 - lax.rem(col, 2)
    far = 1 - near
    per_half = chunks // HALVES

    def mixed_of(first, last, b):
        at = pl.ds(b * chunk, chunk)
        start, stop = needs(first, last)
        inner = lanes_of(start, stop)
        return jnp.dot(
            field[at, inner].astype(BF16), mix[inner, lanes_of(first, last)],
            preferred_element_type=F32,
        )

    def update(first, last, b, mixed):
        at = pl.ds(b * chunk, chunk)
        out = lanes_of(first, last)
        y = yb[at, out] - 0.2 * mixed
        x = jnp.clip(xb[at, out] + 0.5 * y, -1.0, 1.0)
        yb[at, out] = y
        xb[at, out] = x
        return x

    def add_energy(step, first, last, b, mixed):
        own_rows = pl.ds(cells + b * chunk, chunk)
        rounded = jnp.concatenate([wins[step][g, own_rows, :] for g in range(first, last)], axis=1)
        product_sum = (rounded.astype(F32) * mixed).reshape(chunk // 8, 8, mixed.shape[1])
        epart[:, lanes_of(first, last)] += jnp.sum(product_sum, axis=0)

    epart[...] = jnp.zeros(epart.shape, F32)
    late = None
    for step in range(STEPS):
        field[...] = product(step, 1, 0, groups, 0, cells)
        spread()
        for g in range(groups):
            for h in range(HALVES):
                arrived(step, near, g, h)
        field[...] += product(step, 2 * near, 0, groups, 0, cells)
        done = 0
        for g in range(groups):
            for h in range(HALVES):
                arrived(step, far, g, h)
                if step < STEPS - 1 and (g, h) == (2, 0):
                    @pl.when(lax.rem(row, 2) != lax.rem(col, 2))
                    def _():
                        pl.semaphore_signal(gate_sem, inc=1, device_id=device(me + 1 - 2 * lax.rem(col, 2)), device_id_type=MESH)
                field[:, lanes_of(g, g + 1)] += product(step, 2 * far, g, g + 1, h * half, half)
            ready = done
            while ready < groups and needs(ready, ready + 1)[1] <= g + 1:
                ready += 1
            if ready == done:
                continue
            if step < STEPS - 1 and done == 0:
                @pl.when(lax.rem(row, 2) == lax.rem(col, 2))
                def _():
                    pl.semaphore_wait(gate_sem, 1)
            for b in range(chunks):
                mixed = mixed_of(done, ready, b)
                if step == STEPS - 1:
                    add_energy(step, done, ready, b, mixed)
                    if ready == groups:
                        late = done
                        mixed_ref[pl.ds(b * chunk, chunk), lanes_of(done, ready)] = mixed
                    else:
                        update(done, ready, b, mixed)
                    continue
                x = update(done, ready, b, mixed)
                for send in range(done, ready):
                    wins[step + 1][send, pl.ds(cells + b * chunk, chunk), :] = x[
                        :, (send - done) * LANES:(send - done + 1) * LANES
                    ].astype(BF16)
                if (b + 1) % per_half == 0:
                    for send in range(done, ready):
                        for side in (0, 1):
                            halo_copy(step + 1, side, send, b // per_half).start()
            done = ready
        if step < STEPS - 1:
            for b in range(HALVES):
                base(step + 1, b)

    lane_sum = jnp.sum(epart[...], axis=0, keepdims=True)
    shape = (replicas, width)
    group = group_index(lax.broadcasted_iota(jnp.int32, shape, 1), channels, replicas)
    which = lax.broadcasted_iota(jnp.int32, shape, 0)
    share = jnp.sum(jnp.where(group == which, lane_sum, 0.0), axis=1, keepdims=True)
    shape = (replicas, 128)
    lane = lax.broadcasted_iota(jnp.int32, shape, 1)
    which = lax.broadcasted_iota(jnp.int32, shape, 0)
    eall[0] = jnp.sum(jnp.where(lane == which, share, 0.0), axis=0, keepdims=True)

    def energy_copy(d):
        return pltpu.make_async_remote_copy(
            src_ref=eall.at[0],
            dst_ref=eall.at[d],
            send_sem=esend_sem.at[d],
            recv_sem=erecv_sem.at[d],
            device_id=device(lax.rem(me + d, n)),
            device_id_type=MESH,
        )

    while passed[0] <= rounds:
        spread()

    def send_energy(d, carry):
        energy_copy(d).start()
        return carry

    lax.fori_loop(1, n, send_energy, 0)
    for b in range(chunks):
        update(late, groups, b, mixed_ref[pl.ds(b * chunk, chunk), lanes_of(late, groups)])
    for step in range(STEPS):
        for side in (0, 1):
            for g in range(groups):
                for h in range(HALVES):
                    halo_copy(step, side, g, h).wait_send()

    def take_energy(d, carry):
        energy_copy(d).wait()
        return carry

    lax.fori_loop(1, n, take_energy, 0)
    e_out[...] = (jnp.sum(eall[...], axis=0) * scale)[:, :replicas]


def write_kernel(x_in, y_in, e_in, x_out, y_out, e_out, sem):
    x_copy = pltpu.make_async_copy(x_in, x_out, sem.at[0])
    y_copy = pltpu.make_async_copy(y_in, y_out, sem.at[1])
    x_copy.start()
    y_copy.start()
    e_copy = pltpu.make_async_copy(e_in, e_out, sem.at[2])
    e_copy.start()
    x_copy.wait()
    y_copy.wait()
    e_copy.wait()


def local(rows_n, cols_n, positions, momenta, tile_values, tile_rows, tile_cols, tile_count, channel_coupling):
    cells, width = positions.shape
    slots, tile, _ = tile_values.shape
    channels = channel_coupling.shape[0]
    replicas = width // channels
    targets = cells // tile
    wide_s = pl.cdiv(slots, 128) * 128
    wide_c = pl.cdiv(3 * targets * targets, 128) * 128
    groups = width // LANES
    n = rows_n * cols_n
    rounds = max(1, (n // 2 - 1).bit_length())
    vmem = pl.BlockSpec(memory_space=pltpu.VMEM)
    hbm = pl.BlockSpec(memory_space=pltpu.HBM)
    anywhere = pl.BlockSpec(memory_space=pl.ANY)
    scale = 1.0 / float(cells * n * channels) ** 0.5
    x, y, e = pl.pallas_call(
        functools.partial(main_kernel, rows_n, cols_n, channels, scale),
        out_shape=(
            jax.ShapeDtypeStruct((cells, width), F32),
            jax.ShapeDtypeStruct((cells, width), F32),
            jax.ShapeDtypeStruct((1, replicas), F32),
        ),
        in_specs=[hbm] + [hbm] * 6,
        out_specs=(vmem, vmem, vmem),
        scratch_shapes=[
            pltpu.VMEM((groups, 3 * cells, LANES), BF16),
            pltpu.VMEM((groups, 3 * cells, LANES), BF16),
            pltpu.VMEM((slots, tile, tile), BF16),
            pltpu.VMEM((slots + 1, tile, tile), F32),
            pltpu.VMEM((3, cells, cells), BF16),
            pltpu.VMEM((3, cells, cells), F8),
            pltpu.VMEM((cells, width), F32),
            pltpu.VMEM((cells, width), F32),
            pltpu.VMEM((width, width), BF16),
            pltpu.VMEM((width, width), BF16),
            pltpu.VMEM((8, width), F32),
            pltpu.VMEM((n, 1, 128), F32),
            pltpu.SMEM((1,), jnp.int32),
            pltpu.VMEM((1, slots), jnp.int32),
            pltpu.VMEM((1, slots), jnp.int32),
            pltpu.VMEM((channels, channels), BF16),
            pltpu.VMEM((1, wide_s), jnp.int32),
            pltpu.VMEM((1, wide_s), jnp.int32),
            pltpu.VMEM((1, wide_c), jnp.int32),
            pltpu.SMEM((1, wide_s), jnp.int32),
            pltpu.SMEM((1, wide_c), jnp.int32),
            pltpu.SemaphoreType.DMA((groups + 2,)),
            pltpu.SemaphoreType.DMA((4,)),
            pltpu.SemaphoreType.DMA((2,)),
            pltpu.SemaphoreType.REGULAR,
            pltpu.SemaphoreType.REGULAR((rounds, 2)),
            pltpu.SemaphoreType.DMA((STEPS, 2, groups, HALVES)),
            pltpu.SemaphoreType.DMA((STEPS, 2, groups, HALVES)),
            pltpu.SemaphoreType.DMA((n,)),
            pltpu.SemaphoreType.DMA((n,)),
        ],
        compiler_params=pltpu.CompilerParams(
            collective_id=0, has_side_effects=True, vmem_limit_bytes=42 << 20
        ),
        name="steps",
    )(
        tile_count,
        *(
            pltpu.with_memory_space_constraint(a, pltpu.HBM)
            for a in (
                tile_rows.reshape(1, slots), tile_cols.reshape(1, slots),
                channel_coupling, positions, momenta, tile_values,
            )
        )
    )
    x, y, e = pl.pallas_call(
        write_kernel,
        out_shape=(
            jax.ShapeDtypeStruct((cells, width), F32),
            jax.ShapeDtypeStruct((cells, width), F32),
            jax.ShapeDtypeStruct((1, replicas), F32),
        ),
        in_specs=[anywhere, anywhere, anywhere],
        out_specs=(hbm, hbm, hbm),
        scratch_shapes=[pltpu.SemaphoreType.DMA((3,))],
        compiler_params=pltpu.CompilerParams(vmem_limit_bytes=1 << 20),
        name="write",
    )(x, y, e)
    return x, y, e.reshape(replicas)


def solution(mesh):
    return jax.shard_map(
        functools.partial(local, mesh.shape["row"], mesh.shape["col"]),
        mesh=mesh,
        in_specs=(
            P(("groups", "row", "col"), None),
            P(("groups", "row", "col"), None),
            P(("groups", "row", "col"), None, None),
            P(("groups", "row", "col")),
            P(("groups", "row", "col")),
            P(("groups", "row", "col")),
            P(),
        ),
        out_specs=(
            P(("groups", "row", "col"), None),
            P(("groups", "row", "col"), None),
            P("groups"),
        ),
        check_vma=False,
    )
```

```python
import functools

import jax
import jax.numpy as jnp
from jax import lax
from jax.experimental import pallas as pl
from jax.experimental.pallas import tpu as pltpu
from jax.sharding import PartitionSpec as P

STEPS = 2
LANES = 128
HALVES = 2
MESH = pl.DeviceIdType.MESH
F32 = jnp.float32
BF16 = jnp.bfloat16
F8 = jnp.float8_e4m3fn
LOW_SCALE = 4096.0


def group_index(index, channels, replicas):
    group = jnp.zeros(index.shape, jnp.int32)
    for r in range(1, replicas):
        group = group + (index >= r * channels).astype(jnp.int32)
    return group


def main_kernel(
    rows_n, cols_n, channels, scale,
    count_hbm, rows_hbm, cols_hbm, coupling_hbm, x_hbm, y_hbm, v_hbm,
    xb, yb, e_out,
    win0, win1, values, sums, dense_hi, dense_lo, field, mixed_ref, mix, ones, epart, eall,
    count_ref, rows_ref, cols_ref, coupling_ref, keys, prev_v, last_v, prev_ref, last_ref,
    in_sem, small_sem, table_sem, gate_sem, known_sem, send_sem, recv_sem, esend_sem, erecv_sem,
):
    cells, width = xb.shape
    slots, tile, _ = values.shape
    chunk = 4 * tile
    chunks = cells // chunk
    targets = cells // tile
    sources = 3 * targets
    replicas = width // channels
    groups = width // LANES
    half = cells // HALVES
    n = rows_n * cols_n
    wins = (win0, win1)
    row, col = lax.axis_index("row"), lax.axis_index("col")
    me = row * cols_n + col

    def device(flat):
        return {"row": lax.div(flat, cols_n), "col": lax.rem(flat, cols_n)}

    def lanes_of(first, last):
        return pl.ds(first * LANES, (last - first) * LANES)

    def x_copy(g):
        part = lanes_of(g, g + 1)
        return pltpu.make_async_copy(x_hbm.at[:, part], xb.at[:, part], in_sem.at[g])

    v_copy = pltpu.make_async_copy(v_hbm, values, in_sem.at[groups])
    y_copy = pltpu.make_async_copy(y_hbm, yb, in_sem.at[groups + 1])
    small = [
        pltpu.make_async_copy(a, b, small_sem.at[i])
        for i, (a, b) in enumerate(
            (
                (count_hbm, count_ref),
                (rows_hbm, rows_ref),
                (cols_hbm, cols_ref),
                (coupling_hbm, coupling_ref),
            )
        )
    ]
    for g in range(groups):
        x_copy(g).start()
    barrier = pltpu.get_barrier_semaphore()

    def tell(sem, d):
        pl.semaphore_signal(
            sem, inc=1, device_id=device(lax.rem(me + n + d, n)), device_id_type=MESH
        )

    tell(barrier, 1)
    tell(barrier, -1)
    rounds = known_sem.shape[0]
    passed = [0]

    def spread():
        k = passed[0]
        if 0 < k <= rounds:
            for side in (0, 1):
                pl.semaphore_wait(known_sem.at[k - 1, side], 1)
        if k < rounds:
            tell(known_sem.at[k, 0], 1 << k)
            tell(known_sem.at[k, 1], -(1 << k))
        passed[0] = k + 1

    for copy in small:
        copy.start()
    y_copy.start()
    v_copy.start()

    right = device(lax.rem(me + 1, n))
    left = device(lax.rem(me + n - 1, n))

    def halo_copy(step, side, g, h):
        win = wins[step]
        return pltpu.make_async_remote_copy(
            src_ref=win.at[g, pl.ds(cells + h * half, half)],
            dst_ref=win.at[g, pl.ds(2 * cells * side + h * half, half)],
            send_sem=send_sem.at[step, side, g, h],
            recv_sem=recv_sem.at[step, side, g, h],
            device_id=left if side else right,
            device_id_type=MESH,
        )

    def arrived(step, side, g, h):
        win = wins[step]
        pltpu.make_async_remote_copy(
            src_ref=win.at[g, pl.ds(cells + h * half, half)],
            dst_ref=win.at[g, pl.ds(2 * cells * side + h * half, half)],
            send_sem=send_sem.at[step, 0, g, h],
            recv_sem=recv_sem.at[step, side, g, h],
            device_id=right,
            device_id_type=MESH,
        ).wait_recv()

    for g in range(groups):
        x_copy(g).wait()
        win0[g, pl.ds(cells, cells), :] = xb[:, lanes_of(g, g + 1)].astype(BF16)
        if g == 0:
            pl.semaphore_wait(barrier, 2)
        for first in (True, False):
            for side in (0, 1):
                @pl.when((lax.rem(col, 2) != side) == first)
                def _():
                    for h in range(HALVES):
                        halo_copy(0, side, g, h).start()

    spread()
    for copy in small:
        copy.wait()
    lanes = lax.broadcasted_iota(jnp.int32, (1, slots), 1)
    keys[...] = jnp.full(keys.shape, -1, jnp.int32)
    keys[:, :slots] = jnp.where(lanes < count_ref[0], rows_ref[...] * sources + cols_ref[...], -1)
    wide_s, wide_c = prev_v.shape[1], last_v.shape[1]
    first = lax.broadcasted_iota(jnp.int32, (wide_s, wide_s), 0)
    second = lax.broadcasted_iota(jnp.int32, (wide_s, wide_s), 1)
    key_row = keys[...]
    key_col = jnp.sum(jnp.where(first == second, key_row, 0), axis=1, keepdims=True)
    best = jnp.max(
        jnp.where((key_col == key_row) & (first < second), first, -1), axis=0, keepdims=True
    )
    prev_v[...] = jnp.where(best < 0, slots, best)
    slot = lax.broadcasted_iota(jnp.int32, (wide_s, wide_c), 0)
    cell = lax.broadcasted_iota(jnp.int32, (wide_s, wide_c), 1)
    best = jnp.max(jnp.where(key_col == cell, slot, -1), axis=0, keepdims=True)
    last_v[...] = jnp.where(best < 0, slots, best)
    prev_copy = pltpu.make_async_copy(prev_v, prev_ref, table_sem.at[0])
    last_copy = pltpu.make_async_copy(last_v, last_ref, table_sem.at[1])
    prev_copy.start()
    last_copy.start()

    group_r = group_index(lax.broadcasted_iota(jnp.int32, (width, width), 0), channels, replicas)
    group_c = group_index(lax.broadcasted_iota(jnp.int32, (width, width), 1), channels, replicas)
    same = group_r == group_c
    ones[...] = jnp.where(same, 1.0, 0.0).astype(BF16)
    pick_c = lax.broadcasted_iota(jnp.int32, (channels, width), 1)
    pick_c = pick_c - channels * group_index(pick_c, channels, replicas)
    pick = jnp.where(
        pick_c == lax.broadcasted_iota(jnp.int32, (channels, width), 0), 1.0, 0.0
    ).astype(BF16)
    pick_r = lax.broadcasted_iota(jnp.int32, (width, channels), 0)
    pick_r = pick_r - channels * group_index(pick_r, channels, replicas)
    pick_t = jnp.where(
        pick_r == lax.broadcasted_iota(jnp.int32, (width, channels), 1), 1.0, 0.0
    ).astype(BF16)
    wide = jnp.dot(coupling_ref[...], pick, preferred_element_type=F32).astype(BF16)
    full = jnp.dot(pick_t, wide, preferred_element_type=F32)
    mix[...] = jnp.where(same, full, 0.0).astype(BF16)

    def base(step, b):
        at = pl.ds(pl.multiple_of(b * half, half), half)
        x = xb[at, :]
        high = x.astype(BF16)
        low = ((x - high.astype(F32)) * LOW_SCALE).astype(F8)
        totals = jnp.dot(high, ones[...], preferred_element_type=F32) + jnp.dot(
            low, ones[...].astype(F8), preferred_element_type=F32
        ) * (1.0 / LOW_SCALE)
        penalty = 0.02 * (totals - (2.0 - channels))
        detune = 1.0 - (step + 1.0) / (STEPS + 1.0)
        yb[at, :] = yb[at, :] + 0.5 * (-detune * x - 0.4 * penalty)

    def base_loop(b, carry):
        base(0, b)
        return carry

    y_copy.wait()
    lax.fori_loop(0, HALVES, base_loop, 0)
    sums[slots] = jnp.zeros((tile, tile), F32)
    v_copy.wait()
    prev_copy.wait()
    last_copy.wait()

    def add_tile(s, carry):
        sums[s] = sums[prev_ref[0, s]] + values[s].astype(F32)
        return carry

    lax.fori_loop(0, slots, add_tile, 0, unroll=4)

    def place(i, carry):
        p, t = lax.div(i, targets), lax.rem(i, targets)
        at = pl.ds(pl.multiple_of(t * tile, tile), tile)
        for j in range(targets):
            total = sums[last_ref[0, t * sources + p * targets + j]]
            high = total.astype(BF16)
            dense_hi[p, at, j * tile:(j + 1) * tile] = high
            low = (total - high.astype(F32)) * LOW_SCALE
            dense_lo[p, at, j * tile:(j + 1) * tile] = low.astype(F8)
        return carry

    lax.fori_loop(0, 3 * targets, place, 0)
    spread()

    def product(step, block, first, last, start, size):
        rows = pl.ds(pl.multiple_of(block * cells + start, size), size)
        part = pl.ds(start, size)
        source = jnp.concatenate([wins[step][g, rows, :] for g in range(first, last)], axis=1)
        low = jnp.dot(dense_lo[block, :, part], source.astype(F8), preferred_element_type=F32)
        high = jnp.dot(dense_hi[block, :, part], source, preferred_element_type=F32)
        return high + low * (1.0 / LOW_SCALE)

    def needs(first, last):
        start = first * LANES // channels * channels // LANES
        stop = -(-min(-(-last * LANES // channels) * channels, width) // LANES)
        return start, stop

    near = 1 - lax.rem(col, 2)
    far = 1 - near
    per_half = chunks // HALVES

    def mixed_of(first, last, b):
        at = pl.ds(b * chunk, chunk)
        start, stop = needs(first, last)
        inner = lanes_of(start, stop)
        return jnp.dot(
            field[at, inner].astype(BF16), mix[inner, lanes_of(first, last)],
            preferred_element_type=F32,
        )

    def update(first, last, b, mixed):
        at = pl.ds(b * chunk, chunk)
        out = lanes_of(first, last)
        y = yb[at, out] - 0.2 * mixed
        x = jnp.clip(xb[at, out] + 0.5 * y, -1.0, 1.0)
        yb[at, out] = y
        xb[at, out] = x
        return x

    def add_energy(step, first, last, b, mixed):
        own_rows = pl.ds(cells + b * chunk, chunk)
        rounded = jnp.concatenate([wins[step][g, own_rows, :] for g in range(first, last)], axis=1)
        product_sum = (rounded.astype(F32) * mixed).reshape(chunk // 8, 8, mixed.shape[1])
        epart[:, lanes_of(first, last)] += jnp.sum(product_sum, axis=0)

    epart[...] = jnp.zeros(epart.shape, F32)
    late = None
    for step in range(STEPS):
        field[...] = product(step, 1, 0, groups, 0, cells)
        spread()
        for g in range(groups):
            for h in range(HALVES):
                arrived(step, near, g, h)
        field[...] += product(step, 2 * near, 0, groups, 0, cells)
        done = 0
        for g in range(groups):
            for h in range(HALVES):
                arrived(step, far, g, h)
                if step < STEPS - 1 and (g, h) == (2, 0):
                    @pl.when(lax.rem(row, 2) != lax.rem(col, 2))
                    def _():
                        pl.semaphore_signal(gate_sem, inc=1, device_id=device(me + 1 - 2 * lax.rem(col, 2)), device_id_type=MESH)
                field[:, lanes_of(g, g + 1)] += product(step, 2 * far, g, g + 1, h * half, half)
            ready = done
            while ready < groups and needs(ready, ready + 1)[1] <= g + 1:
                ready += 1
            if ready == done:
                continue
            if step < STEPS - 1 and done == 0:
                @pl.when(lax.rem(row, 2) == lax.rem(col, 2))
                def _():
                    pl.semaphore_wait(gate_sem, 1)
            for b in range(chunks):
                mixed = mixed_of(done, ready, b)
                if step == STEPS - 1:
                    add_energy(step, done, ready, b, mixed)
                    if ready == groups:
                        late = done
                        mixed_ref[pl.ds(b * chunk, chunk), lanes_of(done, ready)] = mixed
                    else:
                        update(done, ready, b, mixed)
                    continue
                x = update(done, ready, b, mixed)
                for send in range(done, ready):
                    wins[step + 1][send, pl.ds(cells + b * chunk, chunk), :] = x[
                        :, (send - done) * LANES:(send - done + 1) * LANES
                    ].astype(BF16)
                if (b + 1) % per_half == 0:
                    for send in range(done, ready):
                        for side in (0, 1):
                            halo_copy(step + 1, side, send, b // per_half).start()
            done = ready
        if step < STEPS - 1:
            for b in range(HALVES):
                base(step + 1, b)

    lane_sum = jnp.sum(epart[...], axis=0, keepdims=True)
    shape = (replicas, width)
    group = group_index(lax.broadcasted_iota(jnp.int32, shape, 1), channels, replicas)
    which = lax.broadcasted_iota(jnp.int32, shape, 0)
    share = jnp.sum(jnp.where(group == which, lane_sum, 0.0), axis=1, keepdims=True)
    shape = (replicas, 128)
    lane = lax.broadcasted_iota(jnp.int32, shape, 1)
    which = lax.broadcasted_iota(jnp.int32, shape, 0)
    eall[0] = jnp.sum(jnp.where(lane == which, share, 0.0), axis=0, keepdims=True)

    def energy_copy(d):
        return pltpu.make_async_remote_copy(
            src_ref=eall.at[0],
            dst_ref=eall.at[d],
            send_sem=esend_sem.at[d],
            recv_sem=erecv_sem.at[d],
            device_id=device(lax.rem(me + d, n)),
            device_id_type=MESH,
        )

    while passed[0] <= rounds:
        spread()

    def send_energy(d, carry):
        energy_copy(d).start()
        return carry

    lax.fori_loop(1, n, send_energy, 0)
    for b in range(chunks):
        update(late, groups, b, mixed_ref[pl.ds(b * chunk, chunk), lanes_of(late, groups)])
    for step in range(STEPS):
        for side in (0, 1):
            for g in range(groups):
                for h in range(HALVES):
                    halo_copy(step, side, g, h).wait_send()

    def take_energy(d, carry):
        energy_copy(d).wait()
        return carry

    lax.fori_loop(1, n, take_energy, 0)
    e_out[...] = (jnp.sum(eall[...], axis=0) * scale)[:, :replicas]


def write_kernel(x_in, y_in, e_in, x_out, y_out, e_out, sem):
    x_copy = pltpu.make_async_copy(x_in, x_out, sem.at[0])
    y_copy = pltpu.make_async_copy(y_in, y_out, sem.at[1])
    x_copy.start()
    y_copy.start()
    e_copy = pltpu.make_async_copy(e_in, e_out, sem.at[2])
    e_copy.start()
    x_copy.wait()
    y_copy.wait()
    e_copy.wait()


def local(rows_n, cols_n, positions, momenta, tile_values, tile_rows, tile_cols, tile_count, channel_coupling):
    cells, width = positions.shape
    slots, tile, _ = tile_values.shape
    channels = channel_coupling.shape[0]
    replicas = width // channels
    targets = cells // tile
    wide_s = pl.cdiv(slots, 128) * 128
    wide_c = pl.cdiv(3 * targets * targets, 128) * 128
    groups = width // LANES
    n = rows_n * cols_n
    rounds = max(1, (n // 2 - 1).bit_length())
    vmem = pl.BlockSpec(memory_space=pltpu.VMEM)
    hbm = pl.BlockSpec(memory_space=pltpu.HBM)
    anywhere = pl.BlockSpec(memory_space=pl.ANY)
    scale = 1.0 / float(cells * n * channels) ** 0.5
    x, y, e = pl.pallas_call(
        functools.partial(main_kernel, rows_n, cols_n, channels, scale),
        out_shape=(
            jax.ShapeDtypeStruct((cells, width), F32),
            jax.ShapeDtypeStruct((cells, width), F32),
            jax.ShapeDtypeStruct((1, replicas), F32),
        ),
        in_specs=[hbm] + [hbm] * 6,
        out_specs=(vmem, vmem, vmem),
        scratch_shapes=[
            pltpu.VMEM((groups, 3 * cells, LANES), BF16),
            pltpu.VMEM((groups, 3 * cells, LANES), BF16),
            pltpu.VMEM((slots, tile, tile), BF16),
            pltpu.VMEM((slots + 1, tile, tile), F32),
            pltpu.VMEM((3, cells, cells), BF16),
            pltpu.VMEM((3, cells, cells), F8),
            pltpu.VMEM((cells, width), F32),
            pltpu.VMEM((cells, width), F32),
            pltpu.VMEM((width, width), BF16),
            pltpu.VMEM((width, width), BF16),
            pltpu.VMEM((8, width), F32),
            pltpu.VMEM((n, 1, 128), F32),
            pltpu.SMEM((1,), jnp.int32),
            pltpu.VMEM((1, slots), jnp.int32),
            pltpu.VMEM((1, slots), jnp.int32),
            pltpu.VMEM((channels, channels), BF16),
            pltpu.VMEM((1, wide_s), jnp.int32),
            pltpu.VMEM((1, wide_s), jnp.int32),
            pltpu.VMEM((1, wide_c), jnp.int32),
            pltpu.SMEM((1, wide_s), jnp.int32),
            pltpu.SMEM((1, wide_c), jnp.int32),
            pltpu.SemaphoreType.DMA((groups + 2,)),
            pltpu.SemaphoreType.DMA((4,)),
            pltpu.SemaphoreType.DMA((2,)),
            pltpu.SemaphoreType.REGULAR,
            pltpu.SemaphoreType.REGULAR((rounds, 2)),
            pltpu.SemaphoreType.DMA((STEPS, 2, groups, HALVES)),
            pltpu.SemaphoreType.DMA((STEPS, 2, groups, HALVES)),
            pltpu.SemaphoreType.DMA((n,)),
            pltpu.SemaphoreType.DMA((n,)),
        ],
        compiler_params=pltpu.CompilerParams(
            collective_id=0, has_side_effects=True, vmem_limit_bytes=42 << 20
        ),
        name="steps",
    )(
        tile_count,
        *(
            pltpu.with_memory_space_constraint(a, pltpu.HBM)
            for a in (
                tile_rows.reshape(1, slots), tile_cols.reshape(1, slots),
                channel_coupling, positions, momenta, tile_values,
            )
        )
    )
    x, y, e = pl.pallas_call(
        write_kernel,
        out_shape=(
            jax.ShapeDtypeStruct((cells, width), F32),
            jax.ShapeDtypeStruct((cells, width), F32),
            jax.ShapeDtypeStruct((1, replicas), F32),
        ),
        in_specs=[anywhere, anywhere, anywhere],
        out_specs=(hbm, hbm, hbm),
        scratch_shapes=[pltpu.SemaphoreType.DMA((3,))],
        compiler_params=pltpu.CompilerParams(vmem_limit_bytes=1 << 20),
        name="write",
    )(x, y, e)
    return x, y, e.reshape(replicas)


def solution(mesh):
    return jax.shard_map(
        functools.partial(local, mesh.shape["row"], mesh.shape["col"]),
        mesh=mesh,
        in_specs=(
            P(("groups", "row", "col"), None),
            P(("groups", "row", "col"), None),
            P(("groups", "row", "col"), None, None),
            P(("groups", "row", "col")),
            P(("groups", "row", "col")),
            P(("groups", "row", "col")),
            P(),
        ),
        out_specs=(
            P(("groups", "row", "col"), None),
            P(("groups", "row", "col"), None),
            P("groups"),
        ),
        check_vma=False,
    )
```
